32 devices in a mesh: groups: 2 (over y), ctx: 4 (over z), head: 2 (over x), sub: 2 (over core).
Axes of the slice: x: 2, y: 2, z: 4, core: 2. Of those that a mesh axis runs over, the one named last changes fastest.
Arguments:
- queries: bfloat16 [4096, 8, 8, 128], P(('groups', 'ctx'), 'head', 'sub'), parts along dimension 0, may hold values from -6 to 6
- keys: bfloat16 [4096, 8, 128], P(('groups', 'ctx'), ('head', 'sub')), parts along dimension 0, may hold values from -6 to 6
- values: bfloat16 [4096, 8, 128], P(('groups', 'ctx'), ('head', 'sub')), parts along dimension 0, may hold values from -6 to 6
- span_order: int32 [8], replicated, may hold values from 0 to 7, as said below
Outputs:
- attended: bfloat16 [4096, 8, 8, 128], P(('groups', 'ctx'), 'head', 'sub'), parts along dimension 0
The draws below stay inside these ranges and needn't reach their ends.
There are 2 independent parts, one for each index of `groups`. The reference program is written for one: setup_inputs(seed, part) draws one part's arguments, and reference() takes and returns one part's arrays. A program takes and returns all parts, laid end to end along the dimension named above; an argument that names none is the same for every part. Nothing has to cross between parts.
Inputs may be any that keep to these rules, and one draw needn't show every extreme that they name: `span_order`: each block index appears exactly once, and for every i the stored blocks 2 i and 2 i + 1 hold block indices that sum to 7.
All inputs are finite; a program needn't handle non-finite values.
Results may differ from the reference program's by a relative error of at most 0.0049.
Values may be sent and summed in bfloat16 or wider, within the bound.
A program may use at most 64 MiB of HBM per device.

```python
import math
import jax
import jax.numpy as jnp
from jax import lax

KEY_VALUE_HEADS = 8
QUERIES_PER_KV = 8
HEAD_SIZE = 128
SPAN = 256
SEQUENCE_TOKENS = 2048


def drawn_pair(key):
    query_random_seed = jax.random.fold_in(key, 11)
    key_random_seed = jax.random.fold_in(key, 12)
    sampled_queries = jnp.clip(jax.random.normal(query_random_seed, (SEQUENCE_TOKENS, KEY_VALUE_HEADS, QUERIES_PER_KV, HEAD_SIZE), jnp.float32), -6.0, 6.0)
    sampled_keys = jnp.clip(jax.random.normal(key_random_seed, (SEQUENCE_TOKENS, KEY_VALUE_HEADS, HEAD_SIZE), jnp.float32), -6.0, 6.0)
    return (sampled_queries.astype(jnp.bfloat16), sampled_keys.astype(jnp.bfloat16))


def draw_queries(key, part):
    return drawn_pair(key)[0]


def draw_keys(key, part):
    return drawn_pair(key)[1]


def draw_span_order(key, part):
    cycle_count = SEQUENCE_TOKENS // SPAN // 2
    order_key = jax.random.fold_in(key, 21)
    lower = jax.random.permutation(order_key, cycle_count).astype(jnp.int32)
    upper = (2 * cycle_count - 1 - lower).astype(jnp.int32)
    return jnp.stack((lower, upper), axis=1).reshape(-1).astype(jnp.int32)


def shard_levels(own_key, shape, pieces, smallest, top_value):
    level = 1.0
    for position, shards_of in pieces:
        draws = jax.random.uniform(jax.random.fold_in(jax.random.fold_in(own_key, 6), position), (shards_of,), jnp.float32, smallest / len(pieces), top_value / len(pieces))
        level = level * jnp.repeat(jnp.exp(draws), shape[position] // shards_of).reshape((-1,) + (1,) * (len(shape) - 1 - position))
    return level


def normal_values(stream_key, dims, spread, bound, split=(), kind=jnp.bfloat16):
    entries = jax.random.normal(stream_key, dims, jnp.float32) * spread
    if len(split) > 0:
        entries = shard_levels(stream_key, dims, split, -0.22, 0.18) * entries
    return jnp.clip(entries, min=-bound, max=bound).astype(kind)


def setup_inputs(seed: int = 0, part: int = 0) -> dict:
    streams_of = jax.random.split(jax.random.key(seed), 5)
    part_splits = jax.random.split(jax.random.fold_in(streams_of[4], part), 5)
    queries = draw_queries(jax.random.fold_in(jax.random.fold_in(streams_of[4], part), 71), part)
    keys = draw_keys(jax.random.fold_in(jax.random.fold_in(streams_of[4], part), 71), part)
    values = normal_values(part_splits[2], (SEQUENCE_TOKENS, KEY_VALUE_HEADS, HEAD_SIZE), 1.0, 6.0, ((0, 4), (1, 4)))
    span_order = draw_span_order(jax.random.fold_in(streams_of[4], 71), part)
    return {"queries": queries, "keys": keys, "values": values, "span_order": span_order}


def reference(queries, keys, values, span_order):
    offsets = jnp.arange(SPAN, dtype=jnp.int32)
    positions = (span_order[:, None] * SPAN + offsets[None, :]).reshape(-1).astype(jnp.int32)
    scale = 1.0 / math.sqrt(HEAD_SIZE)
    sequence_blocks = SEQUENCE_TOKENS // SPAN

    def single_head(head_index):
        key_rows = keys[:, head_index, :].astype(jnp.float32)
        value_rows = values[:, head_index, :].astype(jnp.float32)
        query_rows = queries[:, head_index].reshape(sequence_blocks, SPAN, QUERIES_PER_KV, HEAD_SIZE)
        query_pos = positions.reshape(sequence_blocks, SPAN)

        def one_block(inputs):
            query_block, block_pos = inputs
            scores = jnp.einsum('rqd,kd->qrk', query_block.astype(jnp.float32), key_rows, precision=lax.Precision.HIGHEST) * scale
            visible = positions[None, None, :] <= block_pos[None, :, None]
            scores = jnp.where(visible, scores, -1e+30)
            peak = lax.optimization_barrier(jnp.max(scores, axis=-1, keepdims=True))
            weights = jnp.where(visible, jnp.exp(scores - peak), 0.0)
            total = lax.optimization_barrier(jnp.sum(weights, axis=-1))
            rounded = lax.optimization_barrier(weights.astype(jnp.bfloat16)).astype(jnp.float32)
            summed = jnp.einsum('qrk,kd->rqd', rounded, value_rows, precision=lax.Precision.HIGHEST)
            return (summed / jnp.transpose(total)[:, :, None]).astype(jnp.bfloat16)
        result = lax.map(one_block, (query_rows, query_pos))
        return result.reshape(SEQUENCE_TOKENS, QUERIES_PER_KV, HEAD_SIZE)
    stacked_heads = lax.map(single_head, jnp.arange(KEY_VALUE_HEADS, dtype=jnp.int32))
    return jnp.transpose(stacked_heads, (1, 0, 2, 3))
```

```python
import functools
import math

import jax
import jax.numpy as jnp
from jax import lax
from jax.experimental import pallas as pl
from jax.experimental.pallas import tpu as pltpu
from jax.sharding import PartitionSpec as P

MESH = pl.DeviceIdType.MESH
HIDDEN = -1e30


def scores_of(q, k):
    return lax.dot_general(q, k, (((1,), (1,)), ((), ())), preferred_element_type=jnp.float32)


def kernel(
    n, span_ref, q_ref, kv_ref, out_ref, buf, acc, peak, total, send_sem, recv_sem, pair_send, pair_recv
):
    z = lax.axis_index("ctx")
    c = lax.axis_index("sub")
    heads, _, rows, width = kv_ref.shape
    span = rows // 2
    q_rows = q_ref.shape[1] // 2
    per_row = q_rows // span
    factor = math.log2(math.e) / math.sqrt(width)
    has_left, has_right = z > 0, z < n - 1

    def to_left(src, block, h):
        return pltpu.make_async_remote_copy(
            src_ref=src, dst_ref=buf.at[0, block, h], send_sem=send_sem.at[0, block, h],
            recv_sem=recv_sem.at[block, h], device_id={"ctx": z - 1}, device_id_type=MESH)

    def to_right(src, block, h):
        return pltpu.make_async_remote_copy(
            src_ref=src, dst_ref=buf.at[0, block, h], send_sem=send_sem.at[1, block, h],
            recv_sem=recv_sem.at[block, h], device_id={"ctx": z + 1}, device_id_type=MESH)

    def to_pair(src, block, h):
        return pltpu.make_async_remote_copy(
            src_ref=src, dst_ref=buf.at[1, block, h], send_sem=pair_send.at[block, h],
            recv_sem=pair_recv.at[block, h], device_id={"sub": 1 - c}, device_id_type=MESH)

    barrier = pltpu.get_barrier_semaphore()
    pl.semaphore_signal(barrier, inc=1, device_id={"sub": 1 - c}, device_id_type=MESH)

    @pl.when(has_left)
    def _():
        pl.semaphore_signal(barrier, inc=1, device_id={"ctx": z - 1}, device_id_type=MESH)

    @pl.when(has_right)
    def _():
        pl.semaphore_signal(barrier, inc=1, device_id={"ctx": z + 1}, device_id_type=MESH)

    pl.semaphore_wait(barrier, 1 + jnp.where(has_left, 1, 0) + jnp.where(has_right, 1, 0))

    for h in range(heads):
        @pl.when(has_left)
        def _(h=h):
            to_left(kv_ref.at[h], z, h).start()

        @pl.when(has_right)
        def _(h=h):
            to_right(kv_ref.at[h], z, h).start()

        to_pair(kv_ref.at[h], z, h).start()

    my_first, my_second = span_ref[2 * z], span_ref[2 * z + 1]
    my_low = jnp.minimum(my_first, my_second)
    flipped = my_first > my_second

    def halves(ref_value, swap):
        size = ref_value.shape[0] // 2
        first, second = ref_value[:size], ref_value[size:]
        return jnp.where(swap, second, first), jnp.where(swap, first, second)

    def weigh(scores, top):
        return jnp.exp2((scores - top) * factor)

    def row_max(s):
        return jnp.max(s, axis=1, keepdims=True)

    def row_sum(s):
        return jnp.sum(s, axis=1, keepdims=True)

    def mix(w, v):
        return jnp.dot(w.astype(jnp.bfloat16), v, preferred_element_type=jnp.float32)

    def keep(which, g, top, summed, numerator):
        peak[which, g] = jnp.broadcast_to(top, (q_rows, width))
        total[which, g] = jnp.broadcast_to(summed, (q_rows, width))
        acc[which, g] = numerator

    def own_head(k, v, g):
        k_low, k_high = halves(k, flipped)
        v_low, v_high = halves(v, flipped)
        q_low, q_high = halves(q_ref[g], flipped)
        q_at = lax.broadcasted_iota(jnp.int32, (q_rows, span), 0) // per_row
        k_at = lax.broadcasted_iota(jnp.int32, (q_rows, span), 1)
        visible = k_at <= q_at
        s = jnp.where(visible, scores_of(q_low, k_low), HIDDEN)
        top = row_max(s)
        w = weigh(s, top)
        keep(0, g, top, row_sum(w), mix(w, v_low))
        s1 = scores_of(q_high, k_low)
        s2 = jnp.where(visible, scores_of(q_high, k_high), HIDDEN)
        top = row_max(jnp.maximum(s1, s2))
        w1, w2 = weigh(s1, top), weigh(s2, top)
        keep(1, g, top, row_sum(w1 + w2), mix(w1, v_low) + mix(w2, v_high))

    def other_head(k, v, block, g):
        first, second = span_ref[2 * block], span_ref[2 * block + 1]
        below = jnp.minimum(first, second) < my_low
        k_low, k_high = halves(k, first > second)
        v_low, v_high = halves(v, first > second)
        q_low, q_high = halves(q_ref[g], flipped)
        k_pick = jnp.where(below, k_low, k_high)
        v_pick = jnp.where(below, v_low, v_high)
        q_pick = jnp.where(below, q_low, q_high)
        s1 = scores_of(q_high, k_low)
        s2 = scores_of(q_pick, k_pick)
        top1, top2 = row_max(s1), row_max(s2)
        old_low, old_high = peak[0, g], peak[1, g]
        new_low = jnp.where(below, jnp.maximum(old_low, top2), old_low)
        new_high = jnp.maximum(old_high, jnp.where(below, top1, jnp.maximum(top1, top2)))
        w1 = weigh(s1, new_high[:, :1])
        w2 = weigh(s2, jnp.where(below, new_low, new_high)[:, :1])
        sum1, sum2 = row_sum(w1), row_sum(w2)
        o1, o2 = mix(w1, v_low), mix(w2, v_pick)
        r_low, r_high = weigh(old_low, new_low), weigh(old_high, new_high)
        peak[0, g] = new_low
        peak[1, g] = new_high
        total[0, g] = total[0, g] * r_low + jnp.where(below, sum2, 0.0)
        total[1, g] = total[1, g] * r_high + jnp.where(below, sum1, sum1 + sum2)
        acc[0, g] = acc[0, g] * r_low + jnp.where(below, o2, 0.0)
        acc[1, g] = acc[1, g] * r_high + jnp.where(below, o1, o1 + o2)

    def own_step(h, carry):
        own_head(kv_ref[h, 0], kv_ref[h, 1], c * heads + h)
        return carry

    lax.fori_loop(0, heads, own_step, 0)

    def pair_step(h, carry):
        to_pair(kv_ref.at[h], z, h).wait_recv()
        own_head(buf[1, z, h, 0], buf[1, z, h, 1], (1 - c) * heads + h)
        return carry

    lax.fori_loop(0, heads, pair_step, 0)

    def step(index, carry):
        hop = index // heads + 1
        h = index % heads
        left_block, right_block = z - hop, z + hop

        @pl.when(left_block >= 0)
        def _():
            block = left_block
            to_right(buf.at[0, block, h], block, h).wait_recv()

            @pl.when(has_right)
            def _():
                to_right(buf.at[0, block, h], block, h).start()

            to_pair(buf.at[0, block, h], block, h).start()

        @pl.when(right_block < n)
        def _():
            block = right_block
            to_left(buf.at[0, block, h], block, h).wait_recv()

            @pl.when(has_left)
            def _():
                to_left(buf.at[0, block, h], block, h).start()

            to_pair(buf.at[0, block, h], block, h).start()

        def part(which, carry):
            side = which // 2
            block = jnp.where(which % 2 == 0, left_block, right_block)

            @pl.when((block >= 0) & (block < n))
            def _():
                @pl.when(side == 1)
                def _():
                    to_pair(buf.at[0, block, h], block, h).wait_recv()

                core = jnp.where(side == 0, c, 1 - c)
                other_head(buf[side, block, h, 0], buf[side, block, h, 1], block, core * heads + h)

            return carry

        return lax.fori_loop(0, 4, part, carry)

    lax.fori_loop(0, (n - 1) * heads, step, 0)

    def finish(g, carry):
        low = (acc[0, g] / total[0, g]).astype(jnp.bfloat16)
        high = (acc[1, g] / total[1, g]).astype(jnp.bfloat16)
        out_ref[g, :q_rows] = jnp.where(flipped, high, low)
        out_ref[g, q_rows:] = jnp.where(flipped, low, high)
        return carry

    lax.fori_loop(0, 2 * heads, finish, 0)

    def drain(index, carry):
        block = index // heads
        h = index % heads

        @pl.when(has_left & (block >= z))
        def _():
            to_left(buf.at[0, block, h], block, h).wait_send()

        @pl.when(has_right & (block <= z))
        def _():
            to_right(buf.at[0, block, h], block, h).wait_send()

        to_pair(buf.at[0, block, h], block, h).wait_send()
        return carry

    lax.fori_loop(0, n * heads, drain, 0)


def on_device(n, queries, keys, values, span_order):
    rows, groups, per_group, width = queries.shape
    heads = keys.shape[1]
    q = jnp.transpose(queries, (1, 0, 2, 3)).reshape(groups, rows * per_group, width)
    kv = jnp.transpose(jnp.stack((keys, values)), (2, 0, 1, 3))
    state = (2, groups, rows * per_group // 2, width)
    out = pl.pallas_call(
        functools.partial(kernel, n),
        out_shape=jax.ShapeDtypeStruct(q.shape, jnp.bfloat16),
        in_specs=[
            pl.BlockSpec(memory_space=pltpu.SMEM),
            pl.BlockSpec(memory_space=pltpu.VMEM),
            pl.BlockSpec(memory_space=pltpu.VMEM),
        ],
        out_specs=pl.BlockSpec(memory_space=pltpu.VMEM),
        scratch_shapes=[
            pltpu.VMEM((2, n, heads, 2, rows, width), jnp.bfloat16),
            pltpu.VMEM(state, jnp.float32),
            pltpu.VMEM(state, jnp.float32),
            pltpu.VMEM(state, jnp.float32),
            pltpu.SemaphoreType.DMA((2, n, heads)),
            pltpu.SemaphoreType.DMA((n, heads)),
            pltpu.SemaphoreType.DMA((n, heads)),
            pltpu.SemaphoreType.DMA((n, heads)),
        ],
        compiler_params=pltpu.CompilerParams(
            collective_id=0, has_side_effects=True, vmem_limit_bytes=56 * 1024 * 1024),
    )(span_order, q, kv)
    out = out.reshape(groups, rows, per_group, width)
    return jnp.transpose(out, (1, 0, 2, 3))


def solution(mesh):
    return jax.shard_map(
        functools.partial(on_device, mesh.shape["ctx"]),
        mesh=mesh,
        in_specs=(
            P(("groups", "ctx"), "head", "sub", None),
            P(("groups", "ctx"), ("head", "sub"), None),
            P(("groups", "ctx"), ("head", "sub"), None),
            P(),
        ),
        out_specs=P(("groups", "ctx"), "head", "sub", None),
        check_vma=False,
    )
```

```python
import functools
import math

import jax
import jax.numpy as jnp
from jax import lax
from jax.experimental import pallas as pl
from jax.experimental.pallas import tpu as pltpu
from jax.sharding import PartitionSpec as P

MESH = pl.DeviceIdType.MESH
HIDDEN = -1e30
PART_COLS = 1024


def scores_of(q, k):
    return lax.dot_general(q, k, (((1,), (1,)), ((), ())), preferred_element_type=jnp.float32)


def kernel(
    n, span_ref, q_any, k_any, v_any, out_any, q_ref, o_ref, buf, acc, peak, total,
    send_sem, recv_sem, pair_send, pair_recv, own_sem, q_sem, o_sem
):
    z = lax.axis_index("ctx")
    c = lax.axis_index("sub")
    heads, rows, width = k_any.shape
    parts = 2
    groups = 2 * heads
    span = rows // 2
    per_row = q_any.shape[2]
    q_rows = span * per_row
    part_cols = min(q_rows, PART_COLS)
    factor = math.log2(math.e) / math.sqrt(width)
    has_left, has_right = z > 0, z < n - 1

    def to_left(src, block, h, p):
        return pltpu.make_async_remote_copy(
            src_ref=src, dst_ref=buf.at[0, block, h, p], send_sem=send_sem.at[0, block, h, p],
            recv_sem=recv_sem.at[block, h, p], device_id={"ctx": z - 1}, device_id_type=MESH)

    def to_right(src, block, h, p):
        return pltpu.make_async_remote_copy(
            src_ref=src, dst_ref=buf.at[0, block, h, p], send_sem=send_sem.at[1, block, h, p],
            recv_sem=recv_sem.at[block, h, p], device_id={"ctx": z + 1}, device_id_type=MESH)

    def to_pair(src, block, h, p):
        return pltpu.make_async_remote_copy(
            src_ref=src, dst_ref=buf.at[1, block, h, p], send_sem=pair_send.at[block, h, p],
            recv_sem=pair_recv.at[block, h, p], device_id={"sub": 1 - c}, device_id_type=MESH)

    def own_copy(h, p):
        return pltpu.make_async_copy((k_any, v_any)[p].at[h], buf.at[0, z, h, p], own_sem.at[h, p])

    def q_copy(g):
        return pltpu.make_async_copy(q_any.at[:, g], q_ref.at[g], q_sem.at[g])

    def o_copy(g):
        return pltpu.make_async_copy(o_ref.at[g], out_any.at[:, g], o_sem.at[g])

    for h in range(heads):
        for p in range(parts):
            own_copy(h, p).start()

    barrier = pltpu.get_barrier_semaphore()
    pl.semaphore_signal(barrier, inc=1, device_id={"sub": 1 - c}, device_id_type=MESH)

    @pl.when(has_left)
    def _():
        pl.semaphore_signal(barrier, inc=1, device_id={"ctx": z - 1}, device_id_type=MESH)

    @pl.when(has_right)
    def _():
        pl.semaphore_signal(barrier, inc=1, device_id={"ctx": z + 1}, device_id_type=MESH)

    pl.semaphore_wait(barrier, 1 + jnp.where(has_left, 1, 0) + jnp.where(has_right, 1, 0))

    for h in range(heads):
        for p in range(parts):
            src = (k_any, v_any)[p].at[h]

            @pl.when(has_left)
            def _(src=src, h=h, p=p):
                to_left(src, z, h, p).start()

            @pl.when(has_right)
            def _(src=src, h=h, p=p):
                to_right(src, z, h, p).start()

            to_pair(src, z, h, p).start()

    for g in range(groups):
        q_copy(g).start()

    for h in range(heads):
        for p in range(parts):
            own_copy(h, p).wait()

    for g in range(groups):
        q_copy(g).wait()

    my_first, my_second = span_ref[2 * z], span_ref[2 * z + 1]
    my_low = jnp.minimum(my_first, my_second)
    flipped = my_first > my_second

    def halves(ref_value, swap):
        size = ref_value.shape[0] // 2
        first, second = ref_value[:size], ref_value[size:]
        return jnp.where(swap, second, first), jnp.where(swap, first, second)

    def weigh(scores, top):
        return jnp.exp2((scores - top) * factor)

    def row_max(s):
        return jnp.max(s, axis=0, keepdims=True)

    def row_sum(s):
        return jnp.sum(s, axis=0, keepdims=True)

    def mix(w, v):
        return lax.dot_general(
            v, w.astype(jnp.bfloat16), (((0,), (0,)), ((), ())), preferred_element_type=jnp.float32)

    def queries_of(g, start):
        picked = q_ref[g, start // per_row : (start + part_cols) // per_row]
        return picked.reshape(part_cols, width)

    def finish(g):
        low = (acc[0, g] * (1.0 / total[0, g])).astype(jnp.bfloat16).T
        high = (acc[1, g] * (1.0 / total[1, g])).astype(jnp.bfloat16).T
        first, second = jnp.where(flipped, high, low), jnp.where(flipped, low, high)
        o_ref[g, :span] = first.reshape(span, per_row, width)
        o_ref[g, span:] = second.reshape(span, per_row, width)
        o_copy(g).start()

    def own_head(k, v, g):
        k_low, k_high = halves(k, flipped)
        v_low, v_high = halves(v, flipped)
        k_at = lax.broadcasted_iota(jnp.int32, (span, part_cols), 0)
        for start in range(0, q_rows, part_cols):
            cols = slice(start, start + part_cols)
            first, second = queries_of(g, start), queries_of(g, q_rows + start)
            q_low, q_high = jnp.where(flipped, second, first), jnp.where(flipped, first, second)
            q_at = (lax.broadcasted_iota(jnp.int32, (span, part_cols), 1) + start) // per_row
            visible = k_at <= q_at
            s = jnp.where(visible, scores_of(k_low, q_low), HIDDEN)
            top = row_max(s)
            w = weigh(s, top)
            peak[0, g, :, cols] = top
            total[0, g, :, cols] = row_sum(w)
            acc[0, g, :, cols] = mix(w, v_low)
            s1 = scores_of(k_low, q_high)
            s2 = jnp.where(visible, scores_of(k_high, q_high), HIDDEN)
            top = jnp.maximum(row_max(s1), row_max(s2))
            w1, w2 = weigh(s1, top), weigh(s2, top)
            peak[1, g, :, cols] = top
            total[1, g, :, cols] = row_sum(w1) + row_sum(w2)
            acc[1, g, :, cols] = mix(w1, v_low) + mix(w2, v_high)

    def other_head(k, v, block, g):
        first, second = span_ref[2 * block], span_ref[2 * block + 1]
        below = jnp.minimum(first, second) < my_low
        k_low, k_high = halves(k, first > second)
        v_low, v_high = halves(v, first > second)
        k_pick = jnp.where(below, k_low, k_high)
        v_pick = jnp.where(below, v_low, v_high)
        for start in range(0, q_rows, part_cols):
            cols = slice(start, start + part_cols)
            q_first, q_second = queries_of(g, start), queries_of(g, q_rows + start)
            q_high = jnp.where(flipped, q_first, q_second)
            q_pick = jnp.where(flipped == below, q_second, q_first)
            s1 = scores_of(k_low, q_high)
            s2 = scores_of(k_pick, q_pick)
            top1, top2 = row_max(s1), row_max(s2)
            old_low, old_high = peak[0, g, :, cols], peak[1, g, :, cols]
            new_low = jnp.where(below, jnp.maximum(old_low, top2), old_low)
            new_high = jnp.maximum(old_high, jnp.where(below, top1, jnp.maximum(top1, top2)))
            w1 = weigh(s1, new_high)
            w2 = weigh(s2, jnp.where(below, new_low, new_high))
            sum1, sum2 = row_sum(w1), row_sum(w2)
            o1, o2 = mix(w1, v_low), mix(w2, v_pick)
            r_low, r_high = weigh(old_low, new_low), weigh(old_high, new_high)
            peak[0, g, :, cols] = new_low
            peak[1, g, :, cols] = new_high
            total[0, g, :, cols] = total[0, g, :, cols] * r_low + jnp.where(below, sum2, 0.0)
            total[1, g, :, cols] = total[1, g, :, cols] * r_high + jnp.where(below, sum1, sum1 + sum2)
            acc[0, g, :, cols] = acc[0, g, :, cols] * r_low + jnp.where(below, o2, 0.0)
            acc[1, g, :, cols] = acc[1, g, :, cols] * r_high + jnp.where(below, o1, o1 + o2)

    def own_step(h, carry):
        own_head(buf[0, z, h, 0], buf[0, z, h, 1], c * heads + h)
        return carry

    lax.fori_loop(0, heads, own_step, 0)

    def pair_step(h, carry):
        for p in range(parts):
            to_pair(buf.at[0, z, h, p], z, h, p).wait_recv()
        own_head(buf[1, z, h, 0], buf[1, z, h, 1], (1 - c) * heads + h)
        return carry

    lax.fori_loop(0, heads, pair_step, 0)

    def step(index, carry):
        hop = index // heads + 1
        h = index % heads
        left_block, right_block = z - hop, z + hop

        for p in range(parts):
            @pl.when(left_block >= 0)
            def _(p=p):
                block = left_block
                src = buf.at[0, block, h, p]
                to_right(src, block, h, p).wait_recv()

                @pl.when(has_right)
                def _():
                    to_right(src, block, h, p).start()

                to_pair(src, block, h, p).start()

            @pl.when(right_block < n)
            def _(p=p):
                block = right_block
                src = buf.at[0, block, h, p]
                to_left(src, block, h, p).wait_recv()

                @pl.when(has_left)
                def _():
                    to_left(src, block, h, p).start()

                to_pair(src, block, h, p).start()

        def part(which, carry):
            side = which // 2
            block = jnp.where(which % 2 == 0, left_block, right_block)

            @pl.when((block >= 0) & (block < n))
            def _():
                @pl.when(side == 1)
                def _():
                    for p in range(parts):
                        to_pair(buf.at[0, block, h, p], block, h, p).wait_recv()

                core = jnp.where(side == 0, c, 1 - c)
                other_head(buf[side, block, h, 0], buf[side, block, h, 1], block, core * heads + h)

            @pl.when((hop == n - 1) & (which % 2 == 1))
            def _():
                finish(jnp.where(side == 0, c, 1 - c) * heads + h)

            return carry

        return lax.fori_loop(0, 4, part, carry)

    lax.fori_loop(0, (n - 1) * heads, step, 0)

    def drain(index, carry):
        block = index // heads
        h = index % heads
        for p in range(parts):
            src = buf.at[0, block, h, p]

            @pl.when(has_left & (block >= z))
            def _(src=src, p=p):
                to_left(src, block, h, p).wait_send()

            @pl.when(has_right & (block <= z))
            def _(src=src, p=p):
                to_right(src, block, h, p).wait_send()

            to_pair(src, block, h, p).wait_send()
        return carry

    lax.fori_loop(0, n * heads, drain, 0)
    for g in range(groups):
        o_copy(g).wait()


def on_device(n, queries, keys, values, span_order):
    rows, groups, per_group, width = queries.shape
    heads = keys.shape[1]
    q_rows = rows * per_group // 2
    k = jnp.transpose(keys, (1, 0, 2))
    v = jnp.transpose(values, (1, 0, 2))
    anywhere = pl.BlockSpec(memory_space=pl.ANY)
    return pl.pallas_call(
        functools.partial(kernel, n),
        out_shape=jax.ShapeDtypeStruct(queries.shape, jnp.bfloat16),
        in_specs=[pl.BlockSpec(memory_space=pltpu.SMEM), pl.BlockSpec(memory_space=pltpu.HBM), anywhere, anywhere],
        out_specs=anywhere,
        scratch_shapes=[
            pltpu.VMEM((groups, rows, per_group, width), jnp.bfloat16),
            pltpu.VMEM((groups, rows, per_group, width), jnp.bfloat16),
            pltpu.VMEM((2, n, heads, 2, rows, width), jnp.bfloat16),
            pltpu.VMEM((2, groups, width, q_rows), jnp.float32),
            pltpu.VMEM((2, groups, 1, q_rows), jnp.float32),
            pltpu.VMEM((2, groups, 1, q_rows), jnp.float32),
            pltpu.SemaphoreType.DMA((2, n, heads, 2)),
            pltpu.SemaphoreType.DMA((n, heads, 2)),
            pltpu.SemaphoreType.DMA((n, heads, 2)),
            pltpu.SemaphoreType.DMA((n, heads, 2)),
            pltpu.SemaphoreType.DMA((heads, 2)),
            pltpu.SemaphoreType.DMA((groups,)),
            pltpu.SemaphoreType.DMA((groups,)),
        ],
        compiler_params=pltpu.CompilerParams(
            collective_id=0, has_side_effects=True, vmem_limit_bytes=48 * 1024 * 1024),
    )(span_order, queries, k, v)


def solution(mesh):
    return jax.shard_map(
        functools.partial(on_device, mesh.shape["ctx"]),
        mesh=mesh,
        in_specs=(
            P(("groups", "ctx"), "head", "sub", None),
            P(("groups", "ctx"), ("head", "sub"), None),
            P(("groups", "ctx"), ("head", "sub"), None),
            P(),
        ),
        out_specs=P(("groups", "ctx"), "head", "sub", None),
        check_vma=False,
    )
```

```python
import functools
import math

import jax
import jax.numpy as jnp
from jax import lax
from jax.experimental import pallas as pl
from jax.experimental.pallas import tpu as pltpu
from jax.sharding import PartitionSpec as P

MESH = pl.DeviceIdType.MESH
HIDDEN = -1e30
PART_COLS = 1024


def scores_of(q, k):
    return lax.dot_general(q, k, (((1,), (1,)), ((), ())), preferred_element_type=jnp.float32)


def kernel(
    n, span_ref, q_any, k_any, v_any, out_any, q_ref, o_ref, buf, acc, peak, total, weights, rescale,
    send_sem, recv_sem, pair_send, pair_recv, own_sem, q_sem, o_sem
):
    z = lax.axis_index("ctx")
    c = lax.axis_index("sub")
    heads, rows, width = k_any.shape
    parts = 2
    groups = 2 * heads
    span = rows // 2
    per_row = q_any.shape[2]
    q_rows = span * per_row
    part_cols = min(q_rows, PART_COLS)
    factor = math.log2(math.e) / math.sqrt(width)
    has_left, has_right = z > 0, z < n - 1

    def to_left(src, block, h, p):
        return pltpu.make_async_remote_copy(
            src_ref=src, dst_ref=buf.at[0, block, h, p], send_sem=send_sem.at[0, block, h, p],
            recv_sem=recv_sem.at[block, h, p], device_id={"ctx": z - 1}, device_id_type=MESH)

    def to_right(src, block, h, p):
        return pltpu.make_async_remote_copy(
            src_ref=src, dst_ref=buf.at[0, block, h, p], send_sem=send_sem.at[1, block, h, p],
            recv_sem=recv_sem.at[block, h, p], device_id={"ctx": z + 1}, device_id_type=MESH)

    def to_pair(src, block, h, p):
        return pltpu.make_async_remote_copy(
            src_ref=src, dst_ref=buf.at[1, block, h, p], send_sem=pair_send.at[block, h, p],
            recv_sem=pair_recv.at[block, h, p], device_id={"sub": 1 - c}, device_id_type=MESH)

    def own_copy(h, p):
        return pltpu.make_async_copy((k_any, v_any)[p].at[h], buf.at[0, z, h, p], own_sem.at[h, p])

    def q_copy(g):
        return pltpu.make_async_copy(q_any.at[:, g], q_ref.at[g], q_sem.at[g])

    def o_copy(g):
        return pltpu.make_async_copy(o_ref.at[g], out_any.at[:, g], o_sem.at[g])

    for h in range(heads):
        for p in range(parts):
            own_copy(h, p).start()

    barrier = pltpu.get_barrier_semaphore()
    pl.semaphore_signal(barrier, inc=1, device_id={"sub": 1 - c}, device_id_type=MESH)

    @pl.when(has_left)
    def _():
        pl.semaphore_signal(barrier, inc=1, device_id={"ctx": z - 1}, device_id_type=MESH)

    @pl.when(has_right)
    def _():
        pl.semaphore_signal(barrier, inc=1, device_id={"ctx": z + 1}, device_id_type=MESH)

    pl.semaphore_wait(barrier, 1 + jnp.where(has_left, 1, 0) + jnp.where(has_right, 1, 0))

    for h in range(heads):
        for p in range(parts):
            src = (k_any, v_any)[p].at[h]

            @pl.when(has_left)
            def _(src=src, h=h, p=p):
                to_left(src, z, h, p).start()

            @pl.when(has_right)
            def _(src=src, h=h, p=p):
                to_right(src, z, h, p).start()

            to_pair(src, z, h, p).start()

    for g in range(groups):
        q_copy(g).start()

    for h in range(heads):
        for p in range(parts):
            own_copy(h, p).wait()

    for g in range(groups):
        q_copy(g).wait()

    my_first, my_second = span_ref[2 * z], span_ref[2 * z + 1]
    my_low = jnp.minimum(my_first, my_second)
    flipped = my_first > my_second

    def halves(ref_value, swap):
        size = ref_value.shape[0] // 2
        first, second = ref_value[:size], ref_value[size:]
        return jnp.where(swap, second, first), jnp.where(swap, first, second)

    def weigh(scores, top):
        return jnp.exp2((scores - top) * factor)

    def row_max(s):
        return jnp.max(s, axis=0, keepdims=True)

    def row_sum(s):
        return jnp.sum(s, axis=0, keepdims=True)

    def mix(w, v):
        return lax.dot_general(
            v, w.astype(jnp.bfloat16), (((0,), (0,)), ((), ())), preferred_element_type=jnp.float32)

    def queries_of(g, start):
        picked = q_ref[g, start // per_row : (start + part_cols) // per_row]
        return picked.reshape(part_cols, width)

    def finish(g):
        low = (acc[0, g] * (1.0 / total[0, g])).astype(jnp.bfloat16).T
        high = (acc[1, g] * (1.0 / total[1, g])).astype(jnp.bfloat16).T
        first, second = jnp.where(flipped, high, low), jnp.where(flipped, low, high)
        o_ref[g, :span] = first.reshape(span, per_row, width)
        o_ref[g, span:] = second.reshape(span, per_row, width)
        o_copy(g).start()

    def own_head(k, v, g):
        k_low, k_high = halves(k, flipped)
        v_low, v_high = halves(v, flipped)
        k_at = lax.broadcasted_iota(jnp.int32, (span, part_cols), 0)
        for start in range(0, q_rows, part_cols):
            cols = slice(start, start + part_cols)
            first, second = queries_of(g, start), queries_of(g, q_rows + start)
            q_low, q_high = jnp.where(flipped, second, first), jnp.where(flipped, first, second)
            q_at = (lax.broadcasted_iota(jnp.int32, (span, part_cols), 1) + start) // per_row
            visible = k_at <= q_at
            s = jnp.where(visible, scores_of(k_low, q_low), HIDDEN)
            top = row_max(s)
            w = weigh(s, top)
            peak[0, g, :, cols] = top
            total[0, g, :, cols] = row_sum(w)
            acc[0, g, :, cols] = mix(w, v_low)
            s1 = scores_of(k_low, q_high)
            s2 = jnp.where(visible, scores_of(k_high, q_high), HIDDEN)
            top = jnp.maximum(row_max(s1), row_max(s2))
            w1, w2 = weigh(s1, top), weigh(s2, top)
            peak[1, g, :, cols] = top
            total[1, g, :, cols] = row_sum(w1) + row_sum(w2)
            acc[1, g, :, cols] = mix(w1, v_low) + mix(w2, v_high)

    def pick_halves(rows_of_head, block):
        first, second = span_ref[2 * block], span_ref[2 * block + 1]
        below = jnp.minimum(first, second) < my_low
        low, high = halves(rows_of_head, first > second)
        return below, low, jnp.where(below, low, high)

    def other_weights(k, block, g, slot):
        below, k_low, k_pick = pick_halves(k, block)
        for start in range(0, q_rows, part_cols):
            cols = slice(start, start + part_cols)
            q_first, q_second = queries_of(g, start), queries_of(g, q_rows + start)
            q_high = jnp.where(flipped, q_first, q_second)
            q_pick = jnp.where(flipped == below, q_second, q_first)
            s1 = scores_of(k_low, q_high)
            s2 = scores_of(k_pick, q_pick)
            top1, top2 = row_max(s1), row_max(s2)
            old_low, old_high = peak[0, g, :, cols], peak[1, g, :, cols]
            new_low = jnp.where(below, jnp.maximum(old_low, top2), old_low)
            new_high = jnp.maximum(old_high, jnp.where(below, top1, jnp.maximum(top1, top2)))
            w1 = weigh(s1, new_high)
            w2 = weigh(s2, jnp.where(below, new_low, new_high))
            sum1, sum2 = row_sum(w1), row_sum(w2)
            weights[slot, 0, :, cols] = w1.astype(jnp.bfloat16)
            weights[slot, 1, :, cols] = w2.astype(jnp.bfloat16)
            r_low, r_high = weigh(old_low, new_low), weigh(old_high, new_high)
            peak[0, g, :, cols] = new_low
            peak[1, g, :, cols] = new_high
            total[0, g, :, cols] = total[0, g, :, cols] * r_low + jnp.where(below, sum2, 0.0)
            total[1, g, :, cols] = total[1, g, :, cols] * r_high + jnp.where(below, sum1, sum1 + sum2)
            rescale[slot, 0, :, cols] = r_low
            rescale[slot, 1, :, cols] = r_high

    def other_values(v, block, g, slot):
        below, v_low, v_pick = pick_halves(v, block)
        for start in range(0, q_rows, part_cols):
            cols = slice(start, start + part_cols)
            o1, o2 = mix(weights[slot, 0, :, cols], v_low), mix(weights[slot, 1, :, cols], v_pick)
            r_low, r_high = rescale[slot, 0, :, cols], rescale[slot, 1, :, cols]
            acc[0, g, :, cols] = acc[0, g, :, cols] * r_low + jnp.where(below, o2, 0.0)
            acc[1, g, :, cols] = acc[1, g, :, cols] * r_high + jnp.where(below, o1, o1 + o2)

    def own_step(h, carry):
        own_head(buf[0, z, h, 0], buf[0, z, h, 1], c * heads + h)
        return carry

    lax.fori_loop(0, heads, own_step, 0)

    def pair_step(h, carry):
        for p in range(parts):
            to_pair(buf.at[0, z, h, p], z, h, p).wait_recv()
        own_head(buf[1, z, h, 0], buf[1, z, h, 1], (1 - c) * heads + h)
        return carry

    lax.fori_loop(0, heads, pair_step, 0)

    def step(index, carry):
        hop = index // heads + 1
        h = index % heads
        left_block, right_block = z - hop, z + hop

        def relay(p):
            @pl.when(left_block >= 0)
            def _():
                block = left_block
                src = buf.at[0, block, h, p]
                to_right(src, block, h, p).wait_recv()

                @pl.when(has_right)
                def _():
                    to_right(src, block, h, p).start()

                to_pair(src, block, h, p).start()

            @pl.when(right_block < n)
            def _():
                block = right_block
                src = buf.at[0, block, h, p]
                to_left(src, block, h, p).wait_recv()

                @pl.when(has_left)
                def _():
                    to_left(src, block, h, p).start()

                to_pair(src, block, h, p).start()

        def part(p, use, which, carry):
            side = which // 2
            block = jnp.where(which % 2 == 0, left_block, right_block)
            g = jnp.where(side == 0, c, 1 - c) * heads + h

            @pl.when((block >= 0) & (block < n))
            def _():
                @pl.when(side == 1)
                def _():
                    to_pair(buf.at[0, block, h, p], block, h, p).wait_recv()

                use(buf[side, block, h, p], block, g, which)

            if p == 1:
                @pl.when((hop == n - 1) & (which % 2 == 1))
                def _():
                    finish(g)

            return carry

        relay(0)
        lax.fori_loop(0, 4, functools.partial(part, 0, other_weights), 0)
        relay(1)
        return lax.fori_loop(0, 4, functools.partial(part, 1, other_values), carry)

    lax.fori_loop(0, (n - 1) * heads, step, 0)

    def drain(index, carry):
        block = index // heads
        h = index % heads
        for p in range(parts):
            src = buf.at[0, block, h, p]

            @pl.when(has_left & (block >= z))
            def _(src=src, p=p):
                to_left(src, block, h, p).wait_send()

            @pl.when(has_right & (block <= z))
            def _(src=src, p=p):
                to_right(src, block, h, p).wait_send()

            to_pair(src, block, h, p).wait_send()
        return carry

    lax.fori_loop(0, n * heads, drain, 0)
    for g in range(groups):
        o_copy(g).wait()


def on_device(n, queries, keys, values, span_order):
    rows, groups, per_group, width = queries.shape
    heads = keys.shape[1]
    q_rows = rows * per_group // 2
    k = jnp.transpose(keys, (1, 0, 2))
    v = jnp.transpose(values, (1, 0, 2))
    anywhere = pl.BlockSpec(memory_space=pl.ANY)
    return pl.pallas_call(
        functools.partial(kernel, n),
        out_shape=jax.ShapeDtypeStruct(queries.shape, jnp.bfloat16),
        in_specs=[pl.BlockSpec(memory_space=pltpu.SMEM), pl.BlockSpec(memory_space=pltpu.HBM), anywhere, anywhere],
        out_specs=anywhere,
        scratch_shapes=[
            pltpu.VMEM((groups, rows, per_group, width), jnp.bfloat16),
            pltpu.VMEM((groups, rows, per_group, width), jnp.bfloat16),
            pltpu.VMEM((2, n, heads, 2, rows, width), jnp.bfloat16),
            pltpu.VMEM((2, groups, width, q_rows), jnp.float32),
            pltpu.VMEM((2, groups, 1, q_rows), jnp.float32),
            pltpu.VMEM((2, groups, 1, q_rows), jnp.float32),
            pltpu.VMEM((4, 2, rows // 2, q_rows), jnp.bfloat16),
            pltpu.VMEM((4, 2, 1, q_rows), jnp.float32),
            pltpu.SemaphoreType.DMA((2, n, heads, 2)),
            pltpu.SemaphoreType.DMA((n, heads, 2)),
            pltpu.SemaphoreType.DMA((n, heads, 2)),
            pltpu.SemaphoreType.DMA((n, heads, 2)),
            pltpu.SemaphoreType.DMA((heads, 2)),
            pltpu.SemaphoreType.DMA((groups,)),
            pltpu.SemaphoreType.DMA((groups,)),
        ],
        compiler_params=pltpu.CompilerParams(
            collective_id=0, has_side_effects=True, vmem_limit_bytes=48 * 1024 * 1024),
    )(pltpu.with_memory_space_constraint(span_order, pltpu.HBM), pltpu.with_memory_space_constraint(queries, pltpu.HBM), k, v)


def solution(mesh):
    return jax.shard_map(
        functools.partial(on_device, mesh.shape["ctx"]),
        mesh=mesh,
        in_specs=(
            P(("groups", "ctx"), "head", "sub", None),
            P(("groups", "ctx"), ("head", "sub"), None),
            P(("groups", "ctx"), ("head", "sub"), None),
            P(),
        ),
        out_specs=P(("groups", "ctx"), "head", "sub", None),
        check_vma=False,
    )
```
